256 devices in a mesh: dp: 8 (over x, core), expert: 32 (over y, z).
Axes of the slice: x: 4, y: 4, z: 8, core: 2. Of those that a mesh axis runs over, the one named last changes fastest.
Arguments:
- tokens: bfloat16 [32768, 2048], P(('dp', 'expert')), may hold values from -6 to 6
- cotangent: bfloat16 [32768, 2048], P(('dp', 'expert')), may hold values from -6 to 6
- gates: bfloat16 [32768, 8], P(('dp', 'expert')), may hold values from 0.049804688 to 1
- expert_ids: int32 [32768, 8], P(('dp', 'expert')), may hold values from 0 to 27, all different within a row; in each aligned block of 128 rows (0 to 127, 128 to 255, ...) at most 39 rows name the same one
- placement: int32 [32], replicated, may hold values from 0 to 27, as said below
- gate_up: bfloat16 [32, 2048, 2, 384], P('expert'), as said below
- down: bfloat16 [32, 384, 2048], P('expert'), as said below
Outputs:
- mixed: bfloat16 [32768, 2048], P(('dp', 'expert'))
- gate_grads: float32 [32768, 8], P(('dp', 'expert'))
- gate_up_grad: float32 [32, 2048, 2, 384], P('expert', 'dp')
- down_grad: float32 [32, 384, 2048], P('expert', None, 'dp')
The draws below stay inside these ranges and needn't reach their ends.
Inputs may be any that keep to these rules, and one draw needn't show every extreme that they name: `expert_ids`: among the rows of one device no expert is named more than 39 times, and some expert reaches 39 in some device's rows. `placement`: every expert is held by one or two copies; exactly 4 experts are held by two, and two copies of one expert always stand at positions 2j and 2j + 1. `gate_up`: copies of one expert hold equal weights. `down`: copies of one expert hold equal weights.
All inputs are finite; a program needn't handle non-finite values.
Results may differ from the reference program's by a relative error of at most 0.012.
Values may be sent and summed in bfloat16 or wider, within the bound.
No kernel may reach another device: no remote copies, remote signals or barrier semaphores. Data moves between devices by JAX's collectives and lax.ppermute only.
A program may use at most 128 MiB of HBM per device.

```python
import math
import jax
import jax.numpy as jnp
import numpy as np
from jax import lax

D = 2048
FF = 384
TOK_DEV = 128
TOPK = 8
HOT = 4
EXPERTS = 28
CAP = 39
TOKENS = 32768
N_DP = 8
N_EXPERT = 32


def place_table(key):
    pair_key = jax.random.fold_in(key, 701)
    unit_key = jax.random.fold_in(key, 702)
    pairs = N_EXPERT // 2
    order = jax.random.permutation(pair_key, pairs).astype(jnp.int32)
    rank = jnp.zeros((pairs,), jnp.int32).at[order].set(jnp.arange(pairs, dtype=jnp.int32))
    doubled = (rank < HOT).astype(jnp.int32)
    slot_ids = jnp.arange(N_EXPERT, dtype=jnp.int32)
    fresh = 1 - doubled[slot_ids // 2] * (slot_ids % 2)
    unit = jnp.cumsum(fresh) - 1
    labels = jax.random.permutation(unit_key, EXPERTS).astype(jnp.int32)
    return labels[unit]


def draw_placement(key, part):
    return place_table(key)


def expert_values(key, shape, fan_in):
    base = jax.random.normal(key, shape, jnp.float32)
    return base * fan_in ** (-0.5)


def draw_gate_up(key, part):
    table = place_table(key)
    base = expert_values(jax.random.fold_in(key, 703), (EXPERTS, D, 2, FF), D)
    return base[table].astype(jnp.bfloat16)


def draw_down(key, part):
    table = place_table(key)
    base = expert_values(jax.random.fold_in(key, 704), (EXPERTS, FF, D), FF)
    return base[table].astype(jnp.bfloat16)


def levels(rng, extent, cuts, least, largest):
    gain, own = 1.0, jax.random.fold_in(rng, 6)
    for dim, parts in cuts:
        draws = jnp.exp(jax.random.uniform(jax.random.fold_in(own, dim), (parts,), jnp.float32, least / len(cuts), largest / len(cuts)))
        gain = gain * jnp.repeat(draws, extent[dim] // parts).reshape([-1 if axis == dim else 1 for axis in range(len(extent))])
    return gain


def shared_out(own_key, own, number, rows, number_of, top, reach, skew):
    ranking = jax.random.permutation(own_key, number_of)
    packed, ordinary = portions_of(number_of, rows * top, reach, skew, True), portions_of(number_of, rows * top, reach, skew, False)
    places = jnp.arange(number_of)

    def named(sizes, rotation):
        used = int((sizes > 0).sum())
        fixed = max(1, used // 4)
        shifted = fixed + (places - fixed + rotation * (used - fixed)) % max(1, number_of - fixed)
        return jnp.zeros((number_of,), jnp.int32).at[ranking[jnp.where(places < fixed, places, shifted)]].set(jnp.asarray(sizes, jnp.int32))

    sizes = jnp.where(number % 4 == 0, named(packed, number // 4), named(ordinary, number - number // 4 - 1))
    mixed = jax.random.permutation(jax.random.fold_in(own, 3), number_of)
    donor, receiver = mixed[0:number_of // 2 * 2:2], mixed[1:number_of // 2 * 2:2]
    margin = jnp.minimum(sizes[donor] - 1, reach - sizes[receiver]) // 2
    margin = jnp.where((donor == ranking[0]) | (receiver == ranking[0]) | (sizes[receiver] == 0), 0, jnp.maximum(margin, 0))
    shifted = jax.random.randint(jax.random.fold_in(own, 4), (number_of // 2,), 0, 1 << 20) % (margin + 1)
    sizes = sizes.at[donor].add(-shifted).at[receiver].add(shifted)
    items = jnp.searchsorted(jnp.cumsum(sizes), jnp.arange(rows * top), side="right").astype(jnp.int32)
    listing = items.reshape(top, rows).T
    listing = listing[jax.random.permutation(jax.random.fold_in(own, 1), rows)]
    rotation = jax.random.randint(jax.random.fold_in(own, 2), (rows, 1), 0, top)
    return jnp.take_along_axis(listing, (jnp.arange(top)[None, :] + rotation) % top, axis=1)


def portions_of(count, total, bound, skew, full):
    weights = [(1 << 20) // math.isqrt(standing ** skew) + 1 for standing in range(1, count + 1)]
    largest = bound if full else min(bound, max(-(-total // count), total * weights[0] // sum(weights)))
    least = 1 if total - largest >= count - 1 else 0
    holding, spare = [largest] + [least] * (count - 1), total - largest - least * (count - 1)
    while spare > 0:
        candidates = [i for i in range(1, count) if holding[i] < largest] or [i for i in range(1, count) if holding[i] < bound]
        mass, left = sum([weights[i] for i in candidates]), spare
        for i in candidates:
            more = min(bound - holding[i], max(1, left * weights[i] // mass), spare)
            holding[i] = holding[i] + more
            spare = spare - more
    return np.array(holding)


def bell_draw(own_key, shape, width, most, split=(), kind=jnp.bfloat16):
    result = width * jax.random.normal(own_key, shape, jnp.float32)
    if split:
        result = result * levels(own_key, shape, split, -0.22, 0.18)
    return jnp.clip(result, -most, most).astype(kind)


def setup_inputs(seed: int = 0) -> dict:
    key_list = jax.random.split(jax.random.key(seed), 8)
    tokens = bell_draw(key_list[0], (TOKENS, D), 1.0, 6.0, ((0, 256),))
    cotangent = bell_draw(key_list[1], (TOKENS, D), 1.0, 6.0, ((0, 256),))
    gates = jnp.clip(jnp.exp(math.log(1.0) - 2.9996462 * jax.random.uniform(key_list[2], (TOKENS, TOPK), jnp.float32) ** levels(key_list[2], (TOKENS, TOPK), ((0, 256),), -0.2, 0.2)), 0.049804688, 1.0).astype(jnp.bfloat16)
    expert_ids_keys = jax.random.split(jax.random.fold_in(key_list[3], 1), TOKENS // TOK_DEV)
    expert_ids_turns = jax.random.permutation(jax.random.fold_in(key_list[3], 3), TOKENS // TOK_DEV)
    expert_ids = jax.vmap(lambda own, number: shared_out(jax.random.fold_in(key_list[3], 2), own, number, TOK_DEV, EXPERTS, TOPK, CAP, 2))(expert_ids_keys, expert_ids_turns).reshape((TOKENS, TOPK))
    placement = draw_placement(jax.random.fold_in(key_list[7], 71), 0)
    gate_up = draw_gate_up(jax.random.fold_in(key_list[7], 71), 0)
    down = draw_down(jax.random.fold_in(key_list[7], 71), 0)
    return dict(tokens=tokens, cotangent=cotangent, gates=gates, expert_ids=expert_ids, placement=placement, gate_up=gate_up, down=down)


def expert_pass(rows_x, rows_dy, rows_g, w_gu, w_d):
    ff = w_d.shape[0]
    proj = jnp.dot(rows_x, w_gu, preferred_element_type=jnp.float32)
    pre_gate = proj[:, :ff]
    pre_up = proj[:, ff:]
    sig = jax.nn.sigmoid(pre_gate)
    act = pre_gate * sig
    hidden = (act * pre_up).astype(jnp.bfloat16)
    outputs = jnp.dot(hidden, w_d, preferred_element_type=jnp.float32).astype(jnp.bfloat16)
    d_out = (rows_g[:, None].astype(jnp.float32) * rows_dy.astype(jnp.float32)).astype(jnp.bfloat16)
    d_hidden = lax.dot_general(d_out, w_d, (((1,), (1,)), ((), ())), preferred_element_type=jnp.float32)
    slope = sig * (1.0 + pre_gate * (1.0 - sig))
    d_proj = jnp.concatenate([d_hidden * pre_up * slope, d_hidden * act], axis=1).astype(jnp.bfloat16)
    grad_gu = lax.dot_general(rows_x, d_proj, (((0,), (0,)), ((), ())), preferred_element_type=jnp.float32).astype(jnp.bfloat16)
    grad_d = lax.dot_general(hidden, d_out, (((0,), (0,)), ((), ())), preferred_element_type=jnp.float32).astype(jnp.bfloat16)
    return outputs, grad_gu, grad_d


def reference(tokens, cotangent, gates, expert_ids, placement, gate_up, down):
    slots = N_EXPERT
    rows_dev = TOK_DEV * TOPK
    expert_range = jnp.arange(EXPERTS, dtype=jnp.int32)
    slot_range = jnp.arange(slots, dtype=jnp.int32)
    match = placement[None, :] == expert_range[:, None]
    first = jnp.min(jnp.where(match, slot_range[None, :], slots), axis=1).astype(jnp.int32)
    extra = (jnp.sum(match.astype(jnp.int32), axis=1) - 1).astype(jnp.int32)
    token_range = jnp.arange(TOKENS, dtype=jnp.int32)
    parity = (token_range[:, None] + jnp.arange(TOPK, dtype=jnp.int32)[None, :]) % 2
    target = first[expert_ids] + extra[expert_ids] * parity
    per_dev = target.reshape(N_DP, N_EXPERT, rows_dev)
    onehot = (per_dev[..., None] == slot_range).astype(jnp.int32)
    position = jnp.sum((jnp.cumsum(onehot, axis=2) - 1) * onehot, axis=3)
    dest = (per_dev * CAP + position).astype(jnp.int32)
    w_gu_all = gate_up.reshape(slots, D, 2 * FF)
    source = jnp.broadcast_to(jnp.arange(N_EXPERT, dtype=jnp.int32)[:, None], (N_EXPERT, rows_dev))

    def to_slots(buffer):
        return buffer.reshape(N_EXPERT, slots, CAP, -1).transpose(1, 0, 2, 3).reshape(slots, N_EXPERT * CAP, -1)

    def replica(carry, items):
        tok, cot, gat, dst = items
        rows_x = jnp.repeat(tok, TOPK, axis=0).reshape(N_EXPERT, rows_dev, D)
        rows_dy = jnp.repeat(cot, TOPK, axis=0).reshape(N_EXPERT, rows_dev, D)
        rows_g = gat.reshape(N_EXPERT, rows_dev)
        buf_x = jnp.zeros((N_EXPERT, slots * CAP, D), jnp.bfloat16).at[source, dst].set(rows_x)
        buf_dy = jnp.zeros((N_EXPERT, slots * CAP, D), jnp.bfloat16).at[source, dst].set(rows_dy)
        buf_g = jnp.zeros((N_EXPERT, slots * CAP), jnp.bfloat16).at[source, dst].set(rows_g)
        slot_x = to_slots(buf_x)
        slot_dy = to_slots(buf_dy)
        slot_g = to_slots(buf_g[..., None])[..., 0]
        outputs, grad_gu, grad_d = lax.map(lambda a: expert_pass(*a), (slot_x, slot_dy, slot_g, w_gu_all, down))
        back = outputs.reshape(slots, N_EXPERT, CAP, D).transpose(1, 0, 2, 3).reshape(N_EXPERT, slots * CAP, D)
        picked = back[source, dst].reshape(N_EXPERT * TOK_DEV, TOPK, D).astype(jnp.float32)
        mixed = jnp.einsum("tk,tkd->td", gat.astype(jnp.float32), picked).astype(jnp.bfloat16)
        d_gates = jnp.einsum("td,tkd->tk", cot.astype(jnp.float32), picked)
        carry = (carry[0] + grad_gu.astype(jnp.float32), carry[1] + grad_d.astype(jnp.float32))
        return carry, (mixed, d_gates)

    init = (jnp.zeros((slots, D, 2 * FF), jnp.float32), jnp.zeros((slots, FF, D), jnp.float32))
    items = (tokens.reshape(N_DP, N_EXPERT * TOK_DEV, D), cotangent.reshape(N_DP, N_EXPERT * TOK_DEV, D),
             gates.reshape(N_DP, N_EXPERT * TOK_DEV, TOPK), dest)
    totals, (mixed, d_gates) = lax.scan(replica, init, items)
    partner = jnp.bitwise_xor(slot_range, 1)
    same = (placement == placement[partner]).astype(jnp.float32)
    gu_total = totals[0] + same[:, None, None] * totals[0][partner]
    d_total = totals[1] + same[:, None, None] * totals[1][partner]
    return (mixed.reshape(TOKENS, D), d_gates.reshape(TOKENS, TOPK),
            gu_total.reshape(slots, D, 2, FF), d_total)
```

```python
import jax
import jax.numpy as jnp
from jax import lax
from jax.experimental import pallas as pl
from jax.experimental.pallas import tpu as pltpu
from jax.sharding import Mesh, PartitionSpec as P

NY = 4
NZ = 8
BF = jnp.bfloat16
F32 = jnp.float32


def block_width(width):
    return 512 if width % 512 == 0 else width


def dispatch_kernel(stride, tok, dest_ref, x_ref, out_ref):
    pairs = x_ref.shape[0] // (2 * tok)
    rows = lax.broadcasted_iota(jnp.int32, (2 * stride, 2 * tok), 0)
    for p in range(pairs):
        picks = []
        for j in range(NY):
            dest = dest_ref[j : j + 1, 2 * tok * p : 2 * tok * (p + 1)]
            picks.append(jnp.where(rows + 2 * stride * p == dest, 1.0, 0.0).astype(BF))
        got = jnp.dot(
            jnp.concatenate(picks, axis=0),
            x_ref[2 * tok * p : 2 * tok * (p + 1), :],
            preferred_element_type=F32,
        ).astype(BF)
        for j in range(NY):
            out_ref[j, 2 * stride * p : 2 * stride * (p + 1), :] = got[2 * stride * j : 2 * stride * (j + 1), :]


def scaled_dispatch_kernel(stride, tok, dest_ref, gate_ref, x_ref, out_ref, plain_ref):
    pairs = x_ref.shape[0] // (2 * tok)
    rows = lax.broadcasted_iota(jnp.int32, (2 * stride, 2 * tok), 0)
    for p in range(pairs):
        picks, scaled = [], []
        for j in range(NY):
            dest = dest_ref[j : j + 1, 2 * tok * p : 2 * tok * (p + 1)]
            gate = gate_ref[j : j + 1, 2 * tok * p : 2 * tok * (p + 1)]
            hit = rows + 2 * stride * p == dest
            picks.append(jnp.where(hit, 1.0, 0.0).astype(BF))
            scaled.append(jnp.where(hit, jnp.broadcast_to(gate, hit.shape), 0.0).astype(BF))
        got = jnp.dot(
            jnp.concatenate(scaled + picks, axis=0),
            x_ref[2 * tok * p : 2 * tok * (p + 1), :],
            preferred_element_type=F32,
        ).astype(BF)
        for j in range(NY):
            out_ref[j, 2 * stride * p : 2 * stride * (p + 1), :] = got[2 * stride * j : 2 * stride * (j + 1), :]
            i = NY + j
            plain_ref[j, 2 * stride * p : 2 * stride * (p + 1), :] = got[2 * stride * i : 2 * stride * (i + 1), :]


def dispatch(x_all, dest, stride, tok, gate=None):
    total, width = x_all.shape
    wide = block_width(width)
    slots = total // tok * stride
    small = pl.BlockSpec((NY, total), lambda i: (0, 0))
    x_spec = pl.BlockSpec((total, wide), lambda i: (0, i))
    out_spec = pl.BlockSpec((NY, slots, wide), lambda i: (0, 0, i))
    out = jax.ShapeDtypeStruct((NY, slots, width), BF)
    if gate is None:
        return pl.pallas_call(
            lambda *refs: dispatch_kernel(stride, tok, *refs),
            grid=(width // wide,),
            in_specs=[small, x_spec],
            out_specs=out_spec,
            out_shape=out,
            name="dispatch",
        )(dest, x_all)
    return pl.pallas_call(
        lambda *refs: scaled_dispatch_kernel(stride, tok, *refs),
        grid=(width // wide,),
        in_specs=[small, small, x_spec],
        out_specs=(out_spec, out_spec),
        out_shape=(out, out),
        name="dispatch_scaled",
    )(dest, gate, x_all)


def combine_kernel(stride, tok, dest_ref, gate_ref, back_ref, plain_ref, mixed_ref, dots_ref, acc_ref):
    step = pl.program_id(0)
    pairs = mixed_ref.shape[0] // (2 * tok)
    cols = lax.broadcasted_iota(jnp.int32, (2 * tok, 2 * stride), 1)
    lanes = lax.broadcasted_iota(jnp.int32, (2 * stride, 128), 1)

    @pl.when(step == 0)
    def _():
        acc_ref[...] = jnp.zeros_like(acc_ref)

    for p in range(pairs):
        weights, rows = [], []
        for j in range(NY):
            dest = dest_ref[2 * tok * p : 2 * tok * (p + 1), j : j + 1]
            gate = gate_ref[2 * tok * p : 2 * tok * (p + 1), j : j + 1]
            hit = cols + 2 * stride * p == dest
            weights.append(jnp.where(hit, gate, 0.0))
            block = back_ref[j, 2 * stride * p : 2 * stride * (p + 1), :]
            rows.append(block)
            prod = block.astype(F32) * plain_ref[j, 2 * stride * p : 2 * stride * (p + 1), :].astype(F32)
            part = prod[:, :128]
            for c in range(1, prod.shape[1] // 128):
                part = part + prod[:, 128 * c : 128 * (c + 1)]
            acc_ref[j, 2 * stride * p : 2 * stride * (p + 1), :] += part
        lhs = jnp.concatenate(weights, axis=1).astype(BF)
        mixed_ref[2 * tok * p : 2 * tok * (p + 1), :] = jnp.dot(
            lhs, jnp.concatenate(rows, axis=0), preferred_element_type=F32
        ).astype(BF)

    @pl.when(step == pl.num_programs(0) - 1)
    def _():
        for p in range(pairs):
            total = jnp.zeros((2 * tok, 128), F32)
            for j in range(NY):
                dest = dest_ref[2 * tok * p : 2 * tok * (p + 1), j : j + 1]
                hit = jnp.where(cols + 2 * stride * p == dest, 1.0, 0.0).astype(BF)
                val = jnp.sum(acc_ref[j, 2 * stride * p : 2 * stride * (p + 1), :], axis=1, keepdims=True)
                high = val.astype(BF)
                low = (val - high.astype(F32)).astype(BF)
                rhs = jnp.where(lanes == j, high.astype(F32), 0.0) + jnp.where(lanes == j + NY, low.astype(F32), 0.0)
                total = total + jnp.dot(hit, rhs.astype(BF), preferred_element_type=F32)
            dots_ref[2 * tok * p : 2 * tok * (p + 1), :] = total


def combine(back, plain, dest_col, gate_col, stride, tok):
    _, slots, width = back.shape
    total = dest_col.shape[0]
    wide = block_width(width)
    small = pl.BlockSpec((total, NY), lambda i: (0, 0))
    big = pl.BlockSpec((NY, slots, wide), lambda i: (0, 0, i))
    return pl.pallas_call(
        lambda *refs: combine_kernel(stride, tok, *refs),
        grid=(width // wide,),
        in_specs=[small, small, big, big],
        out_specs=(
            pl.BlockSpec((total, wide), lambda i: (0, i)),
            pl.BlockSpec((total, 128), lambda i: (0, 0)),
        ),
        out_shape=(
            jax.ShapeDtypeStruct((total, width), BF),
            jax.ShapeDtypeStruct((total, 128), F32),
        ),
        scratch_shapes=[pltpu.VMEM((NY, slots, 128), F32)],
        name="combine",
    )(dest_col, gate_col, back, plain)


def on_device(tokens, cotangent, gates, expert_ids, placement, gate_up, down):
    tok, width = tokens.shape
    topk = expert_ids.shape[1]
    copies = placement.shape[0]
    experts = copies - copies // 8
    capacity = tok * topk * 17 // (16 * experts) + 1
    stride = (capacity + 7) // 8 * 8
    ff = down.shape[1]
    total = NZ * tok

    meta = jnp.concatenate([expert_ids.T.astype(BF), gates.T], axis=0)
    meta_all = lax.all_gather(meta, "ez", axis=0, tiled=False)
    x_all = lax.all_gather(tokens, "ez", axis=0, tiled=True)
    y_all = lax.all_gather(cotangent, "ez", axis=0, tiled=True)

    z = lax.axis_index("ez")
    table = placement.reshape(NY, NZ)
    z_range = jnp.arange(NZ, dtype=jnp.int32)
    mine = jnp.sum(jnp.where(z_range == z, table, 0), axis=1)
    other = jnp.sum(jnp.where(z_range == jnp.bitwise_xor(z, 1), table, 0), axis=1)
    primary = jnp.logical_not(jnp.logical_and(mine == other, z % 2 == 1))
    ids_all = meta_all[:, :topk, :].astype(F32)
    gate_all = meta_all[:, topk:, :].astype(F32)
    chosen = ids_all[None] == mine.astype(F32)[:, None, None, None]
    mask = jnp.any(chosen, axis=2)
    gate_of = jnp.sum(jnp.where(chosen, gate_all[None], 0.0), axis=2)
    t_range = jnp.arange(tok, dtype=jnp.int32)
    before = (t_range[:, None] < t_range[None, :]).astype(BF)
    position = jnp.dot(mask.astype(BF).reshape(NY * NZ, tok), before, preferred_element_type=F32)
    position = position.astype(jnp.int32).reshape(NY, NZ, tok)
    dest = jnp.where(mask, position + stride * z_range[None, :, None], -1).reshape(NY, total)
    gate_of = gate_of.reshape(NY, total)
    dest_col = dest.T
    gate_col = jnp.where(primary[:, None], gate_of, 0.0).T

    send_x = dispatch(x_all, dest, stride, tok)
    recv_x = lax.all_to_all(send_x, "ey", split_axis=0, concat_axis=0, tiled=True)
    send_dy, plain = dispatch(y_all, dest, stride, tok, gate_of)
    recv_dy = lax.all_to_all(send_dy, "ey", split_axis=0, concat_axis=0, tiled=True)

    w_gu = gate_up[0].reshape(width, 2 * ff)
    w_d = down[0]
    rows = NY * NZ * stride
    rows_x = recv_x.reshape(rows, width)
    proj = jnp.dot(rows_x, w_gu, preferred_element_type=F32)
    pre_gate = proj[:, :ff]
    pre_up = proj[:, ff:]
    sig = jax.nn.sigmoid(pre_gate)
    act = pre_gate * sig
    hidden = (act * pre_up).astype(BF)
    outputs = jnp.dot(hidden, w_d, preferred_element_type=F32).astype(BF)
    back = lax.all_to_all(
        outputs.reshape(NY, NZ * stride, width), "ey", split_axis=0, concat_axis=0, tiled=True
    )

    d_out = recv_dy.reshape(rows, width)
    d_hidden = lax.dot_general(d_out, w_d, (((1,), (1,)), ((), ())), preferred_element_type=F32)
    slope = sig * (1.0 + pre_gate * (1.0 - sig))
    d_proj = jnp.concatenate([d_hidden * pre_up * slope, d_hidden * act], axis=1).astype(BF)
    grad_gu = lax.dot_general(
        rows_x, d_proj, (((0,), (0,)), ((), ())), preferred_element_type=F32
    ).astype(BF)
    grad_d = lax.dot_general(
        hidden, d_out, (((0,), (0,)), ((), ())), preferred_element_type=F32
    ).astype(BF)
    total_gu = lax.psum_scatter(grad_gu, "dp", scatter_dimension=0, tiled=True).astype(F32)
    total_d = lax.psum_scatter(grad_d, "dp", scatter_dimension=1, tiled=True).astype(F32)

    mixed_part, dots = combine(back, plain, dest_col, gate_col, stride, tok)
    mixed = lax.psum_scatter(mixed_part, "ez", scatter_dimension=0, tiled=True)
    dots = (dots[:, :NY] + dots[:, NY : 2 * NY]).T.reshape(NY, NZ, 1, tok)
    use = jnp.logical_and(chosen, primary[:, None, None, None])
    d_gates = jnp.sum(jnp.where(use, dots, 0.0), axis=0)
    d_gates = lax.psum_scatter(d_gates, "ez", scatter_dimension=0, tiled=False)
    return (
        mixed,
        d_gates.T,
        total_gu.reshape(1, total_gu.shape[0], 2, ff),
        total_d.reshape(1, ff, total_d.shape[1]),
    )


def solution(mesh):
    split = Mesh(mesh.devices.reshape(mesh.shape["dp"], NY, NZ), ("dp", "ey", "ez"))
    tokens = P(("dp", "ey", "ez"), None)
    return jax.shard_map(
        on_device,
        mesh=split,
        in_specs=(
            tokens,
            tokens,
            tokens,
            tokens,
            P(),
            P(("ey", "ez"), None, None, None),
            P(("ey", "ez"), None, None),
        ),
        out_specs=(
            tokens,
            tokens,
            P(("ey", "ez"), "dp", None, None),
            P(("ey", "ez"), None, "dp"),
        ),
        check_vma=False,
    )
```

```python
import jax
import jax.numpy as jnp
from jax import lax
from jax.experimental import pallas as pl
from jax.experimental.pallas import tpu as pltpu
from jax.sharding import Mesh, PartitionSpec as P


NY = 4
NZ = 8
GROUPS = ((-1, 1, 0), (-2, 2), (-3, 3, 4))
UNITS = ((2, 1), (2,), (2, 1))
EXTRA = 128
BF = jnp.bfloat16
F32 = jnp.float32


def shifted(value, axis, by):
    size = lax.axis_size(axis)
    return lax.ppermute(value, axis, [(i, (i + by) % size) for i in range(size)])


def stacked(blocks):
    if len(blocks) == 1:
        return blocks[0]
    if any(v.shape[0] % 16 for v in blocks):
        return jnp.concatenate([v.astype(F32) for v in blocks], axis=0).astype(blocks[0].dtype)
    return jnp.concatenate(blocks, axis=0)


def gather_ring(value):
    half = value.shape[0] // 2
    got = {0: (value,)}
    up = down = value
    for s in (1, 2, 3):
        up = shifted(up, "ez", 1)
        down = shifted(down, "ez", -1)
        got[-s] = (up,)
        got[s] = (down,)
    got[4] = (shifted(up[:half], "ez", 1), shifted(down[half:], "ez", -1))
    return got


def dispatch_kernel(stride, tok, scaled, parts, units, *refs):
    refs = list(refs)
    dest_ref = refs.pop(0)
    gate_ref = refs.pop(0) if scaled else None
    sources = []
    for n in parts:
        sources.append(stacked([refs.pop(0)[...] for _ in range(n)]))
    outs, plains = refs[:NY], refs[NY:]
    at = 0
    for n in units:
        rows = lax.broadcasted_iota(jnp.int32, (n * stride, n * tok), 0) + stride * at
        cols = slice(tok * at, tok * (at + n))
        picks, gated = [], []
        for j in range(NY):
            hit = rows == dest_ref[j : j + 1, cols]
            picks.append(jnp.where(hit, 1.0, 0.0))
            if scaled:
                gate = jnp.broadcast_to(gate_ref[j : j + 1, cols], hit.shape)
                gated.append(jnp.where(hit, gate, 0.0))
        got = jnp.dot(
            jnp.concatenate(gated + picks, axis=0).astype(BF),
            stacked(sources[at : at + n]),
            preferred_element_type=F32,
        )
        for i, out in enumerate(outs + plains):
            out[stride * at : stride * (at + n), :] = got[n * stride * i : n * stride * (i + 1), :].astype(BF)
        at += n


def dispatch(sources, units, dest, stride, tok, gate=None):
    scaled = gate is not None
    width = sources[0][0].shape[1]
    wide = 512 if width % 512 == 0 else width
    flat = [v for s in sources for v in s]
    small = pl.BlockSpec(dest.shape, lambda i: (0, 0))
    count = 2 * NY if scaled else NY
    rows = len(sources) * stride
    return pl.pallas_call(
        lambda *refs: dispatch_kernel(stride, tok, scaled, [len(s) for s in sources], units, *refs),
        grid=(width // wide,),
        in_specs=[small] * (1 + scaled) + [pl.BlockSpec((v.shape[0], wide), lambda i: (0, i)) for v in flat],
        out_specs=[pl.BlockSpec((rows, wide), lambda i: (0, i))] * count,
        out_shape=[jax.ShapeDtypeStruct((rows, width), BF)] * count,
        name="dispatch_scaled" if scaled else "dispatch",
    )(dest, *([gate] if scaled else []), *flat)


def forward_kernel(*refs):
    xs, (gu_ref, d_ref), refs = refs[:NY], refs[NY : NY + 2], refs[NY + 2 :]
    outs, proj_ref, hidden_ref = refs[:NY], refs[NY], refs[NY + 1]
    ff = d_ref.shape[0]
    size = outs[0].shape[0]
    x = stacked([ref[...] for ref in xs])
    proj = jnp.dot(x, gu_ref[...], preferred_element_type=F32)
    proj_ref[...] = proj
    pre_gate = proj[:, :ff]
    hidden = pre_gate * jax.nn.sigmoid(pre_gate) * proj[:, ff:]
    hidden_ref[...] = hidden.T.astype(BF)
    out = jnp.dot(hidden.astype(BF), d_ref[...], preferred_element_type=F32).astype(BF)
    for j in range(NY):
        outs[j][...] = out[size * j : size * (j + 1), :]


def forward(xs, w_gu, w_d):
    rows = NY * xs[0].shape[0]
    ff = w_d.shape[0]
    return pl.pallas_call(
        forward_kernel,
        out_shape=[jax.ShapeDtypeStruct(x.shape, BF) for x in xs]
        + [jax.ShapeDtypeStruct((rows, 2 * ff), F32), jax.ShapeDtypeStruct((ff, rows), BF)],
        name="forward",
    )(*xs, w_gu, w_d)


def slope_kernel(*refs):
    dys, (d_ref, proj_ref, out_ref) = refs[:NY], refs[NY:]
    ff = d_ref.shape[0]
    dy = stacked([ref[...] for ref in dys])
    d_hidden = lax.dot_general(dy, d_ref[...], (((1,), (1,)), ((), ())), preferred_element_type=F32)
    pre_gate = proj_ref[:, :ff]
    sig = jax.nn.sigmoid(pre_gate)
    out_ref[:ff, :] = (d_hidden * proj_ref[:, ff:] * (sig * (1.0 + pre_gate * (1.0 - sig)))).T.astype(BF)
    out_ref[ff:, :] = (d_hidden * (pre_gate * sig)).T.astype(BF)


def slopes(dys, w_d, proj):
    return pl.pallas_call(
        slope_kernel,
        out_shape=jax.ShapeDtypeStruct(proj.shape[::-1], BF),
        name="slopes",
    )(*dys, w_d, proj)


def grads_kernel(groups, base, order_ref, *refs):
    refs = list(refs)
    xs, dys, das, hs = ([refs.pop(0) for _ in range(n)] for n in (NY * groups, NY * groups, groups, groups))
    base_ref = refs.pop(0) if base else None
    out_ref = refs.pop(0)
    cut = das[0].shape[0]
    for left, right, lo, hi in ((das, xs, 0, cut), (hs, dys, cut, out_ref.shape[1])):
        total = base_ref[0, lo:hi, :] if base else None
        for g in range(groups):
            rhs = stacked([ref[...] for ref in right[NY * g : NY * (g + 1)]])
            part = jnp.dot(left[g][...], rhs, preferred_element_type=F32)
            total = part if total is None else total + part
        out_ref[0, lo:hi, :] = total.astype(out_ref.dtype)


def grads(order, xs, dys, das, hs, tile, dtype, base=None, skip=0):
    steps = order.shape[0]
    rows = das[0].shape[0] + hs[0].shape[0]
    moving = [pl.BlockSpec((v.shape[0], tile), lambda i, o: (0, o[i])) for v in xs + dys]
    fixed = [pl.BlockSpec(v.shape, lambda i, o: (0, 0)) for v in das + hs]
    start = [] if base is None else [pl.BlockSpec((1, rows, tile), lambda i, o: (i + skip, 0, 0))]
    return pl.pallas_call(
        lambda *refs: grads_kernel(len(das), base is not None, *refs),
        grid_spec=pltpu.PrefetchScalarGridSpec(
            num_scalar_prefetch=1,
            grid=(steps,),
            in_specs=moving + fixed + start,
            out_specs=pl.BlockSpec((1, rows, tile), lambda i, o: (i, 0, 0)),
        ),
        out_shape=jax.ShapeDtypeStruct((steps, rows, tile), dtype),
        name="grads",
    )(order, *xs, *dys, *das, *hs, *([] if base is None else [base]))


def total_kernel(*refs):
    parts, gu_ref, d_ref = refs[:-2], refs[-2], refs[-1]
    cut = gu_ref.shape[1]
    total = parts[0][...].astype(F32)
    for ref in parts[1:]:
        total = total + ref[...].astype(F32)
    gu_ref[...] = total[:cut, :].T
    d_ref[...] = total[cut:, :]


def combine_kernel(low, size, split, *refs):
    use_ref, dest_ref, gate_ref, ids_ref = refs[:4]
    backs, plains, outs = refs[4 : 4 + NY], refs[4 + NY : 4 + 2 * NY], refs[4 + 2 * NY :]
    tokens = dest_ref.shape[0]
    width = backs[0].shape[1]
    cols = lax.broadcasted_iota(jnp.int32, (tokens, NY * size), 1)
    lanes = lax.broadcasted_iota(jnp.int32, (size, EXTRA), 1)
    weights = jnp.zeros((tokens, NY * size), F32)
    picks = jnp.zeros((tokens, NY * size), F32)
    sums = []
    for j in range(NY):
        dest = dest_ref[:, j : j + 1] - low
        dest = jnp.where((dest >= 0) & (dest < size), dest + size * j, -1)
        hit = cols == dest
        weights = jnp.where(hit, gate_ref[:, j : j + 1], weights)
        picks = jnp.where(hit, 1.0, picks)
        part = jnp.zeros((size, 128), F32)
        for c in range(width // 128):
            part = part + (
                backs[j][low : low + size, 128 * c : 128 * (c + 1)].astype(F32)
                * plains[j][low : low + size, 128 * c : 128 * (c + 1)].astype(F32)
            )
        val = jnp.sum(part, axis=1, keepdims=True)
        high = val.astype(BF).astype(F32)
        sums.append(jnp.where(lanes == j, high, jnp.where(lanes == j + NY, val - high, 0.0)))
    weights = weights.astype(BF)
    dots = jnp.dot(picks.astype(BF), jnp.concatenate(sums, axis=0).astype(BF), preferred_element_type=F32)
    value = jnp.zeros((tokens, EXTRA), F32)
    for j in range(NY):
        dot = dots[:, j : j + 1] + dots[:, NY + j : NY + j + 1]
        value = jnp.where(ids_ref[...] == use_ref[j], dot, value)
    high = value.astype(BF).astype(F32)
    lane = lax.broadcasted_iota(jnp.int32, (tokens, EXTRA), 1)
    value = jnp.where(lane < EXTRA // 2, high, value - high).astype(BF)
    wide = 512 if width % 512 == 0 else width
    for i, out in enumerate(outs):
        out[:, width:] = value[split * i : split * (i + 1), :]
    for lo in range(0, width, wide):
        rhs = stacked([back[low : low + size, lo : lo + wide] for back in backs])
        block = jnp.dot(weights, rhs, preferred_element_type=F32).astype(BF)
        for i, out in enumerate(outs):
            out[:, lo : lo + wide] = block[split * i : split * (i + 1), :]


def combine(use, tables, backs, plains, low, size, split):
    dest, gate, ids = tables
    tokens = dest.shape[0]
    width = backs[0].shape[1]
    vmem = pl.BlockSpec(memory_space=pltpu.VMEM)
    return pl.pallas_call(
        lambda *refs: combine_kernel(low, size, split, *refs),
        in_specs=[pl.BlockSpec(memory_space=pltpu.SMEM)] + [vmem] * (3 + 2 * NY),
        out_shape=[jax.ShapeDtypeStruct((split, width + EXTRA), BF)] * (tokens // split),
        name="combine",
    )(use, dest, gate, ids, *backs, *plains)


def plus(*values):
    return sum(v.astype(F32) for v in values)


def on_device(tokens, cotangent, gates, expert_ids, placement, gate_up, down):
    tok, width = tokens.shape
    topk = expert_ids.shape[1]
    copies = placement.shape[0]
    experts = copies - copies // 8
    capacity = tok * topk * 17 // (16 * experts) + 1
    stride = (capacity + 7) // 8 * 8
    ff = down.shape[1]
    order = [s for group in GROUPS for s in group]
    y, z = lax.axis_index("ey"), lax.axis_index("ez")

    meta = jnp.concatenate([expert_ids.T.astype(BF), gates.T], axis=0)
    meta_all = lax.all_to_all(
        jnp.broadcast_to(meta[None], (NZ,) + meta.shape), "ez", split_axis=0, concat_axis=0, tiled=True
    )
    x_ring = gather_ring(tokens)
    y_ring = gather_ring(cotangent)

    ranks = (z + jnp.array(order, jnp.int32)) % NZ
    meta_all = meta_all[ranks]
    copy_range = jnp.arange(copies, dtype=jnp.int32)
    rel = (y + jnp.arange(NY, dtype=jnp.int32)) % NY * NZ + z
    mine = jnp.sum(jnp.where(copy_range == rel[:, None], placement, 0), axis=1)
    other = jnp.sum(jnp.where(copy_range == jnp.bitwise_xor(rel, 1)[:, None], placement, 0), axis=1)
    primary = jnp.logical_not(jnp.logical_and(mine == other, rel % 2 == 1))
    use = jnp.where(primary, mine, -2)
    ids_all = meta_all[:, :topk, :].astype(F32)
    gate_all = meta_all[:, topk:, :].astype(F32)
    chosen = ids_all[None] == mine.astype(F32)[:, None, None, None]
    mask = jnp.any(chosen, axis=2)
    gate_of = jnp.sum(jnp.where(chosen, gate_all[None], 0.0), axis=2)
    t_range = jnp.arange(tok, dtype=jnp.int32)
    before = (t_range[:, None] < t_range[None, :]).astype(BF)
    position = jnp.dot(mask.astype(BF).reshape(NY * NZ, tok), before, preferred_element_type=F32)
    position = position.astype(jnp.int32).reshape(NY, NZ, tok)
    start = jnp.array([stride * i for group in GROUPS for i in range(len(group))], jnp.int32)
    dest = jnp.where(mask, position + start[None, :, None], -1)
    ends = [sum(len(group) for group in GROUPS[:g]) for g in range(len(GROUPS) + 1)]
    dest_row = [dest[:, a:b].reshape(NY, -1) for a, b in zip(ends, ends[1:])]
    gate_row = [gate_of[:, a:b].reshape(NY, -1) for a, b in zip(ends, ends[1:])]
    dest_col = dest.transpose(1, 2, 0)
    gate_col = jnp.where(primary[:, None, None], gate_of, 0.0).transpose(1, 2, 0)
    ids_col = ids_all.transpose(0, 2, 1).astype(jnp.int32)
    ids_col = jnp.pad(ids_col, ((0, 0), (0, 0), (0, EXTRA // 2 - topk)), constant_values=-1)
    ids_col = jnp.concatenate([ids_col, ids_col], axis=2)

    def tables(*sources):
        at = [order.index(s) for s in sources]
        return tuple(
            v[at[0]] if len(at) == 1 else v[at[0] : at[0] + 2].reshape(2 * tok, -1)
            for v in (dest_col, gate_col, ids_col)
        )

    w_gu = gate_up[0].reshape(width, 2 * ff)
    w_d = down[0]

    def sent_over_y(blocks, sign):
        out = [blocks[0]]
        for j in range(1, NY):
            out.append(shifted(blocks[j], "ey", sign * j))
        return out

    xs, dys, plains, backs, projs, hs, das = [], [], [], [], [], [], []
    for g, group in enumerate(GROUPS):
        sent = dispatch([x_ring[s] for s in group], UNITS[g], dest_row[g], stride, tok)
        xs.append(sent_over_y(sent, 1))
        sent = dispatch([y_ring[s] for s in group], UNITS[g], dest_row[g], stride, tok, gate_row[g])
        plains.append(sent[NY:])
        dys.append(sent_over_y(sent, 1))
        *outs, proj, hidden = forward(xs[g], w_gu, w_d)
        projs.append(proj)
        hs.append(hidden)
        backs.append(sent_over_y(outs, -1))
        das.append(slopes(dys[g], w_d, projs[g]))

    dp = lax.axis_index("dp")
    devices = lax.axis_size("dp")
    tile = width // devices
    turns = devices // 2
    own_order = (dp + 2 * jnp.arange(turns, dtype=jnp.int32)) % devices
    other_order = jnp.bitwise_xor(own_order, 1)
    early = len(GROUPS) - 1
    base = grads(
        jnp.concatenate([other_order, own_order]),
        sum(xs[:early], []), sum(dys[:early], []), das[:early], hs[:early], tile, F32,
    )
    give = grads(other_order, xs[early], dys[early], das[early:], hs[early:], tile, BF, base)
    taken = lax.ppermute(give, "dp", [(i, i ^ 1) for i in range(devices)])
    keep = grads(own_order, xs[early], dys[early], das[early:], hs[early:], tile, BF, base, turns)
    parts = [keep[0], taken[0]]
    for k in range(1, turns):
        parts.append(shifted(plus(keep[k], taken[k]).astype(BF), "dp", 2 * k))
    total_gu, total_d = pl.pallas_call(
        total_kernel,
        out_shape=[jax.ShapeDtypeStruct((tile, 2 * ff), F32), jax.ShapeDtypeStruct((ff, tile), F32)],
        name="total",
    )(*parts)

    def hop(up, down_):
        return shifted(up, "ez", -1), shifted(down_, "ez", 1)

    pair = 2 * stride
    up, down_ = combine(use, tables(4), backs[2], plains[2], pair, stride, tok // 2)
    up, down_ = hop(up, down_)
    for g, s in ((2, 3), (1, 2), (0, 1)):
        own_up, own_down = combine(use, tables(-s, s), backs[g], plains[g], 0, pair, tok)
        if s == 3:
            half = tok // 2
            up = jnp.concatenate([plus(own_up[:half], up).astype(BF), own_up[half:]], axis=0)
            down_ = jnp.concatenate([own_down[:half], plus(own_down[half:], down_).astype(BF)], axis=0)
        else:
            up, down_ = plus(own_up, up).astype(BF), plus(own_down, down_).astype(BF)
        up, down_ = hop(up, down_)
    (own,) = combine(use, tables(0), backs[0], plains[0], pair, stride, tok)
    whole = plus(own, up, down_)
    mixed = whole[:, :width].astype(BF)
    extra = whole[:, width:]
    d_gates = extra[:, :topk] + extra[:, EXTRA // 2 : EXTRA // 2 + topk]
    return (
        mixed,
        d_gates,
        total_gu.reshape(1, tile, 2, ff),
        total_d.reshape(1, ff, tile),
    )


def solution(mesh):
    split = Mesh(mesh.devices.reshape(mesh.shape["dp"], NY, NZ), ("dp", "ey", "ez"))
    tokens = P(("dp", "ey", "ez"), None)
    return jax.shard_map(
        on_device,
        mesh=split,
        in_specs=(
            tokens,
            tokens,
            tokens,
            tokens,
            P(),
            P(("ey", "ez"), None, None, None),
            P(("ey", "ez"), None, None),
        ),
        out_specs=(
            tokens,
            tokens,
            P(("ey", "ez"), "dp", None, None),
            P(("ey", "ez"), None, "dp"),
        ),
        check_vma=False,
    )
```

```python
import jax
import jax.numpy as jnp
from jax import lax
from jax.experimental import pallas as pl
from jax.experimental.pallas import tpu as pltpu
from jax.sharding import Mesh, PartitionSpec as P


NY = 4
NZ = 8
GROUPS = ((-1, 1, 0), (-2, 2), (-3, 3, 4))
UNITS = ((2, 1), (2,), (2, 1))
DY_GROUPS = ((-2, 2, -1, 1, 0), (-3, 3, 4))
DY_UNITS = ((2, 2, 1), (2, 1))
STAGES = ((1, 0), (2,))
EXTRA = 128
BF = jnp.bfloat16
F32 = jnp.float32


def shifted(value, axis, by):
    size = lax.axis_size(axis)
    return lax.ppermute(value, axis, [(i, (i + by) % size) for i in range(size)])


def stacked(blocks):
    if len(blocks) == 1:
        return blocks[0]
    if any(v.shape[0] % 16 for v in blocks):
        return jnp.concatenate([v.astype(F32) for v in blocks], axis=0).astype(blocks[0].dtype)
    return jnp.concatenate(blocks, axis=0)


def gather_ring(value, split):
    half = value.shape[0] // 2
    got = {0: [value]}
    up = down = value
    for s in (1, 2, 3):
        up = shifted(up, "ez", 1)
        down = shifted(down, "ez", -1)
        got[-s] = [up]
        got[s] = [down]
    if split:
        got[4] = [shifted(up[:half], "ez", 1), shifted(down[half:], "ez", -1)]
    else:
        got[4] = [shifted(down, "ez", -1)]
    return got


def route_kernel(stride, topk, at_ref, place_ref, meta_ref, use_ref, table_ref, *rows_refs):
    y, z = at_ref[0], at_ref[1]
    tok = meta_ref.shape[2]
    mine, primary = [], []
    for j in range(NY):
        copy = (y + j) % NY * NZ + z
        mine.append(place_ref[copy])
        second = jnp.logical_and(place_ref[copy] == place_ref[copy ^ 1], copy % 2 == 1)
        primary.append(jnp.logical_not(second))
        use_ref[j] = jnp.where(second, -2, place_ref[copy])
    masks, gates, ids = [], [], []
    for group in GROUPS:
        for s in group:
            block = meta_ref[(z + (s + NZ)) % NZ].astype(F32)
            names, weights = block[:topk], block[topk:]
            ids.append(names)
            for j in range(NY):
                hit = names == mine[j].astype(F32)
                masks.append(jnp.sum(jnp.where(hit, 1.0, 0.0), axis=0, keepdims=True))
                gates.append(jnp.sum(jnp.where(hit, weights, 0.0), axis=0, keepdims=True))
    first = lax.broadcasted_iota(jnp.int32, (tok, tok), 0)
    before = jnp.where(first < lax.broadcasted_iota(jnp.int32, (tok, tok), 1), 1.0, 0.0).astype(BF)
    mask = jnp.concatenate(masks, axis=0)
    position = jnp.dot(mask.astype(BF), before, preferred_element_type=F32)
    order = [s for group in GROUPS for s in group]

    def rows_of(i, n):
        chosen = mask[NY * i : NY * (i + 1)] > 0.0
        return jnp.where(chosen, position[NY * i : NY * (i + 1)] + float(stride * n), -1.0)

    refs = list(rows_refs)
    for group in GROUPS:
        dest_ref = refs.pop(0)
        for n, s in enumerate(group):
            i = order.index(s)
            dest = rows_of(i, n)
            dest_ref[:, tok * n : tok * (n + 1)] = dest
            gate = gates[NY * i : NY * (i + 1)]
            kept = [jnp.where(primary[j], gate[j], 0.0) for j in range(NY)]
            pad = jnp.full((EXTRA // 2 - topk - 2 * NY, tok), -1.0, F32)
            tall = jnp.concatenate([ids[i], dest, *kept, pad, ids[i], dest, *kept, pad], axis=0)
            table_ref[tok * i : tok * (i + 1), :] = tall.T
    for group in DY_GROUPS:
        dest_ref, gate_ref = refs.pop(0), refs.pop(0)
        for n, s in enumerate(group):
            i = order.index(s)
            dest_ref[:, tok * n : tok * (n + 1)] = rows_of(i, n)
            gate_ref[:, tok * n : tok * (n + 1)] = jnp.concatenate(gates[NY * i : NY * (i + 1)], axis=0)


def route(at, placement, meta, stride, topk):
    tok = meta.shape[2]
    smem, vmem = pl.BlockSpec(memory_space=pltpu.SMEM), pl.BlockSpec(memory_space=pltpu.VMEM)
    shapes = [jax.ShapeDtypeStruct((NY,), jnp.int32), jax.ShapeDtypeStruct((NZ * tok, EXTRA), F32)]
    for group in GROUPS:
        shapes += [jax.ShapeDtypeStruct((NY, len(group) * tok), F32)]
    for group in DY_GROUPS:
        shapes += [jax.ShapeDtypeStruct((NY, len(group) * tok), F32)] * 2
    return pl.pallas_call(
        lambda *refs: route_kernel(stride, topk, *refs),
        in_specs=[smem, smem, vmem],
        out_specs=[smem] + [vmem] * (len(shapes) - 1),
        out_shape=shapes,
        name="route",
    )(at, placement, meta)


def dispatch_kernel(stride, tok, scaled, parts, units, *refs):
    refs = list(refs)
    dest_ref = refs.pop(0)
    gate_ref = refs.pop(0) if scaled else None
    sources = [stacked([refs.pop(0)[...] for _ in range(n)]) for n in parts]
    outs, plains = refs[:NY], refs[NY:]
    at = 0
    for n in units:
        rows = (lax.broadcasted_iota(jnp.int32, (n * stride, n * tok), 0) + stride * at).astype(F32)
        cols = slice(tok * at, tok * (at + n))
        picks, gated = [], []
        for j in range(NY):
            hit = rows == dest_ref[j : j + 1, cols]
            picks.append(jnp.where(hit, 1.0, 0.0))
            if scaled:
                gate = jnp.broadcast_to(gate_ref[j : j + 1, cols], hit.shape)
                gated.append(jnp.where(hit, gate, 0.0))
        got = jnp.dot(
            jnp.concatenate(gated + picks, axis=0).astype(BF),
            stacked(sources[at : at + n]),
            preferred_element_type=F32,
        )
        for i, out in enumerate(outs + plains):
            out[stride * at : stride * (at + n), :] = got[n * stride * i : n * stride * (i + 1), :].astype(BF)
        at += n


def dispatch(sources, units, dest, stride, tok, gate=None):
    scaled = gate is not None
    width = sources[0][0].shape[1]
    flat = [v for s in sources for v in s]
    wide = 512 if width % 512 == 0 else width
    small = pl.BlockSpec(dest.shape, lambda i: (0, 0))
    count = 2 * NY if scaled else NY
    rows = len(sources) * stride
    return pl.pallas_call(
        lambda *refs: dispatch_kernel(stride, tok, scaled, [len(s) for s in sources], units, *refs),
        grid=(width // wide,),
        in_specs=[small] * (1 + scaled) + [pl.BlockSpec((v.shape[0], wide), lambda i: (0, i)) for v in flat],
        out_specs=[pl.BlockSpec((rows, wide), lambda i: (0, i))] * count,
        out_shape=[jax.ShapeDtypeStruct((rows, width), BF)] * count,
        name="dispatch_scaled" if scaled else "dispatch",
    )(dest, *([gate] if scaled else []), *flat)


def forward_kernel(count, *refs):
    xs, (gu_ref, d_ref), outs = refs[:count], refs[count : count + 2], refs[count + 2 : 2 * count + 2]
    proj_ref, hidden_ref = refs[2 * count + 2 :]
    ff = d_ref.shape[0]
    x = stacked([ref[...] for ref in xs])
    proj = jnp.dot(x, gu_ref[...], preferred_element_type=F32)
    proj_ref[...] = proj
    pre_gate = proj[:, :ff]
    hidden = pre_gate * jax.nn.sigmoid(pre_gate) * proj[:, ff:]
    hidden_ref[...] = hidden.T.astype(BF)
    out = jnp.dot(hidden.astype(BF), d_ref[...], preferred_element_type=F32)
    at = 0
    for ref in outs:
        ref[...] = out[at : at + ref.shape[0], :].astype(BF)
        at += ref.shape[0]


def forward(xs, w_gu, w_d):
    rows = sum(x.shape[0] for x in xs)
    ff = w_d.shape[0]
    return pl.pallas_call(
        lambda *refs: forward_kernel(len(xs), *refs),
        out_shape=[jax.ShapeDtypeStruct(x.shape, BF) for x in xs]
        + [jax.ShapeDtypeStruct((rows, 2 * ff), F32), jax.ShapeDtypeStruct((ff, rows), BF)],
        name="forward",
    )(*xs, w_gu, w_d)


def slope_kernel(*refs):
    dys, (d_ref, proj_ref, out_ref) = refs[:NY], refs[NY:]
    ff = d_ref.shape[0]
    dy = stacked([ref[...] for ref in dys])
    d_hidden = lax.dot_general(dy, d_ref[...], (((1,), (1,)), ((), ())), preferred_element_type=F32)
    pre_gate = proj_ref[:, :ff]
    sig = jax.nn.sigmoid(pre_gate)
    out_ref[:ff, :] = (d_hidden * proj_ref[:, ff:] * (sig * (1.0 + pre_gate * (1.0 - sig)))).T.astype(BF)
    out_ref[ff:, :] = (d_hidden * (pre_gate * sig)).T.astype(BF)


def slopes(dys, w_d, proj):
    return pl.pallas_call(
        slope_kernel,
        out_shape=jax.ShapeDtypeStruct(proj.shape[::-1], BF),
        name="slopes",
    )(*dys, w_d, proj)


def grads_kernel(counts, at_ref, *refs):
    refs = list(refs)
    xs, dys = ([[refs.pop(0) for _ in range(n)] for n in side] for side in counts)
    das, hs = ([refs.pop(0) for _ in side] for side in counts)
    out_ref = refs.pop(0)
    cut = das[0].shape[0]
    for left, right, lo, hi in ((das, xs, 0, cut), (hs, dys, cut, out_ref.shape[1])):
        total = None
        for lhs, rhs in zip(left, right):
            part = jnp.dot(lhs[...], stacked([ref[...] for ref in rhs]), preferred_element_type=F32)
            total = part if total is None else total + part
        out_ref[0, lo:hi, :] = total.astype(out_ref.dtype)


def grads(at, flip, devices, xs, dys, das, hs, tile):
    steps = devices // 2
    rows = das[0].shape[0] + hs[0].shape[0]
    counts = [[len(v) for v in side] for side in (xs, dys)]
    flat = [v for side in (xs, dys) for vs in side for v in vs]
    moving = [pl.BlockSpec((v.shape[0], tile), lambda i, o: (0, (o[2] + 2 * i) % devices ^ flip)) for v in flat]
    fixed = [pl.BlockSpec(v.shape, lambda i, o: (0, 0)) for v in das + hs]
    return pl.pallas_call(
        lambda *refs: grads_kernel(counts, *refs),
        grid_spec=pltpu.PrefetchScalarGridSpec(
            num_scalar_prefetch=1,
            grid=(steps,),
            in_specs=moving + fixed,
            out_specs=pl.BlockSpec((1, rows, tile), lambda i, o: (i, 0, 0)),
        ),
        out_shape=jax.ShapeDtypeStruct((steps, rows, tile), BF),
        name="grads",
    )(at, *flat, *das, *hs)


def total_kernel(*refs):
    parts, gu_ref, d_ref = refs[:-2], refs[-2], refs[-1]
    cut = gu_ref.shape[1]
    total = parts[0][...].astype(F32)
    for ref in parts[1:]:
        total = total + ref[...].astype(F32)
    gu_ref[...] = total[:cut, :].T
    d_ref[...] = total[cut:, :]


def combine_kernel(stride, tok, topk, start, skip, units, came, *refs):
    use_ref, table_ref = refs[:2]
    backs, plains = refs[2 : 2 + NY], refs[2 + NY : 2 + 2 * NY]
    arrived, outs = refs[2 + 2 * NY : 2 + 2 * NY + came], refs[2 + 2 * NY + came :]
    rows, width = backs[0].shape
    wide = 512 if width % 512 == 0 else width
    lanes = lax.broadcasted_iota(jnp.int32, (rows, EXTRA), 1)
    sums = []
    for j in range(NY):

        def dotted(c, part):
            at = pl.ds(pl.multiple_of(c * 128, 128), 128)
            return part + backs[j][:, at].astype(F32) * plains[j][skip : skip + rows, at].astype(F32)

        part = lax.fori_loop(0, width // 128, dotted, jnp.zeros((rows, 128), F32))
        val = jnp.sum(part, axis=1, keepdims=True)
        high = val.astype(BF).astype(F32)
        sums.append(jnp.where(lanes == j, high, jnp.where(lanes == j + NY, val - high, 0.0)))
    at = 0
    for n in units:
        low, size, count = stride * at, stride * n, tok * n
        table = table_ref[tok * (start + at) : tok * (start + at + n), :]
        cols = lax.broadcasted_iota(jnp.int32, (count, NY * size), 1).astype(F32)
        weights = jnp.zeros((count, NY * size), F32)
        picks = jnp.zeros((count, NY * size), F32)
        for j in range(NY):
            dest = table[:, topk + j : topk + j + 1]
            dest = jnp.where(dest >= 0.0, dest + float(size * j - low), -1.0)
            hit = cols == dest
            weights = jnp.where(hit, table[:, topk + NY + j : topk + NY + j + 1], weights)
            picks = jnp.where(hit, 1.0, picks)
        weights = weights.astype(BF)
        dots = jnp.dot(
            picks.astype(BF),
            jnp.concatenate([v[low : low + size] for v in sums], axis=0).astype(BF),
            preferred_element_type=F32,
        )
        value = jnp.zeros((count, EXTRA), F32)
        for j in range(NY):
            dot = dots[:, j : j + 1] + dots[:, NY + j : NY + j + 1]
            value = jnp.where(table == use_ref[j].astype(F32), dot, value)
        high = value.astype(BF).astype(F32)
        lane = lax.broadcasted_iota(jnp.int32, (count, EXTRA), 1)
        value = jnp.where(lane % (EXTRA // 2) < topk, jnp.where(lane < EXTRA // 2, high, value - high), 0.0)

        def write(place, block):
            for i in range(n):
                piece = block[tok * i : tok * (i + 1), :]
                if at + i < came:
                    piece = piece + arrived[at + i][:, place].astype(F32)
                outs[at + i][:, place] = piece.astype(BF)

        def mixed(c, _):
            place = pl.ds(pl.multiple_of(c * wide, 128), wide)
            rhs = stacked([back[low : low + size, place] for back in backs])
            write(place, jnp.dot(weights, rhs, preferred_element_type=F32))
            return _

        write(slice(width, width + EXTRA), value)
        lax.fori_loop(0, width // wide, mixed, 0)
        at += n


def combine(use, table, backs, plains, stride, tok, topk, start, skip, units, arrived=()):
    width = backs[0].shape[1]
    smem, vmem = pl.BlockSpec(memory_space=pltpu.SMEM), pl.BlockSpec(memory_space=pltpu.VMEM)
    return pl.pallas_call(
        lambda *refs: combine_kernel(stride, tok, topk, start, skip, units, len(arrived), *refs),
        in_specs=[smem] + [vmem] * (1 + 2 * NY + len(arrived)),
        out_shape=[jax.ShapeDtypeStruct((tok, width + EXTRA), BF)] * sum(units),
        name="combine",
    )(use, table, *backs, *plains, *arrived)


def plus(*values):
    return sum(v.astype(F32) for v in values)


def on_device(tokens, cotangent, gates, expert_ids, placement, gate_up, down):
    tok, width = tokens.shape
    topk = expert_ids.shape[1]
    copies = placement.shape[0]
    experts = copies - copies // 8
    capacity = tok * topk * 17 // (16 * experts) + 1
    stride = (capacity + 7) // 8 * 8
    ff = down.shape[1]
    at = jnp.stack([lax.axis_index(name).astype(jnp.int32) for name in ("ey", "ez", "dp")])

    meta = jnp.concatenate([expert_ids.T.astype(BF), gates.T], axis=0)
    meta_all = lax.all_to_all(
        jnp.broadcast_to(meta[None], (NZ,) + meta.shape), "ez", split_axis=0, concat_axis=0, tiled=True
    )
    x_ring = gather_ring(tokens, True)
    y_ring = gather_ring(cotangent, False)
    use, table, *rows = route(at, placement, meta_all, stride, topk)
    dests, dy_rows = rows[: len(GROUPS)], rows[len(GROUPS) :]
    w_gu = gate_up[0].reshape(width, 2 * ff)
    w_d = down[0]

    def sent_over_y(blocks, sign):
        out = [blocks[0]]
        for j in range(1, NY):
            out.append(shifted(blocks[j], "ey", sign * j))
        return out

    blocks, backs = [], [None] * len(GROUPS)
    for g, group in enumerate(GROUPS):
        sent = dispatch([x_ring[s] for s in group], UNITS[g], dests[g], stride, tok)
        blocks.append(sent_over_y(sent, 1))
    xs, dys, plains, hs, das = [], [], [], [], []
    for n, stage in enumerate(STAGES):
        sent = dispatch([y_ring[s] for s in DY_GROUPS[n]], DY_UNITS[n], dy_rows[2 * n], stride, tok, dy_rows[2 * n + 1])
        plains.append(sent[NY:])
        dys.append(sent_over_y(sent, 1))
        xs.append([blocks[g][j] for j in range(NY) for g in stage])
        *outs, proj, hidden = forward(xs[n], w_gu, w_d)
        hs.append(hidden)
        for i, g in enumerate(stage):
            backs[g] = sent_over_y(outs[i :: len(stage)], -1)
        das.append(slopes(dys[n], w_d, proj))

    devices = lax.axis_size("dp")
    tile = width // devices
    turns = devices // 2
    every = xs, dys, das, hs, tile
    give = grads(at, 1, devices, *every)
    taken = lax.ppermute(give, "dp", [(i, i ^ 1) for i in range(devices)])
    keep = grads(at, 0, devices, *every)
    parts = [keep[0], taken[0]]
    for k in range(1, turns):
        parts.append(shifted(plus(keep[k], taken[k]).astype(BF), "dp", 2 * k))
    total_gu, total_d = pl.pallas_call(
        total_kernel,
        out_shape=[jax.ShapeDtypeStruct((tile, 2 * ff), F32), jax.ShapeDtypeStruct((ff, tile), F32)],
        name="total",
    )(*parts)

    def hop(up, down_):
        return shifted(up, "ez", -1), shifted(down_, "ez", 1)

    def partials(g, plain, skip, arrived=()):
        start = sum(len(group) for group in GROUPS[:g])
        return combine(use, table, backs[g], plain, stride, tok, topk, start, skip, UNITS[g], arrived)

    up, down_, far = partials(2, plains[1], 0)
    up, down_ = hop(up, down_)
    far = shifted(far, "ez", 4)
    up, down_ = hop(*partials(1, plains[0], 0, (up, down_)))
    up, down_, own = partials(0, plains[0], 2 * stride, (up, down_))
    up, down_ = hop(up, down_)
    whole = plus(own, far, up, down_)
    mixed = whole[:, :width].astype(BF)
    extra = whole[:, width:]
    d_gates = extra[:, :topk] + extra[:, EXTRA // 2 : EXTRA // 2 + topk]
    return (
        mixed,
        d_gates,
        total_gu.reshape(1, tile, 2, ff),
        total_d.reshape(1, ff, tile),
    )


def solution(mesh):
    split = Mesh(mesh.devices.reshape(mesh.shape["dp"], NY, NZ), ("dp", "ey", "ez"))
    tokens = P(("dp", "ey", "ez"), None)
    return jax.shard_map(
        on_device,
        mesh=split,
        in_specs=(
            tokens,
            tokens,
            tokens,
            tokens,
            P(),
            P(("ey", "ez"), None, None, None),
            P(("ey", "ez"), None, None),
        ),
        out_specs=(
            tokens,
            tokens,
            P(("ey", "ez"), "dp", None, None),
            P(("ey", "ez"), None, "dp"),
        ),
        check_vma=False,
    )
```

```python
import jax
import jax.numpy as jnp
from jax import lax
from jax.experimental import pallas as pl
from jax.experimental.pallas import tpu as pltpu
from jax.sharding import Mesh, PartitionSpec as P


NY = 4
NZ = 8
GROUPS = ((-1, 1, 0), (-2, 2), (-3, 3, 4))
UNITS = ((2, 1), (2,), (2, 1))
DY_GROUPS = ((-2, 2, -1, 1, 0), (-3, 3, 4))
DY_UNITS = ((2, 2, 1), (2, 1))
STAGES = ((1, 0), (2,))
EXTRA = 128
BF = jnp.bfloat16
F32 = jnp.float32


def shifted(value, axis, by):
    size = lax.axis_size(axis)
    return lax.ppermute(value, axis, [(i, (i + by) % size) for i in range(size)])


def stacked(blocks):
    if len(blocks) == 1:
        return blocks[0]
    if any(v.shape[0] % 16 for v in blocks):
        return jnp.concatenate([v.astype(F32) for v in blocks], axis=0).astype(blocks[0].dtype)
    return jnp.concatenate(blocks, axis=0)


def gather_ring(value, split):
    half = value.shape[0] // 2
    got = {0: [value]}
    up = down = value
    for s in (1, 2, 3):
        up = shifted(up, "ez", 1)
        down = shifted(down, "ez", -1)
        got[-s] = [up]
        got[s] = [down]
    if split:
        got[4] = [shifted(up[:half], "ez", 1), shifted(down[half:], "ez", -1)]
    else:
        got[4] = [shifted(down, "ez", -1)]
    return got


def route_kernel(stride, topk, at_ref, place_ref, meta_ref, use_ref, table_ref, *rows_refs):
    y, z = at_ref[0], at_ref[1]
    tok = meta_ref.shape[2]
    mine, primary = [], []
    for j in range(NY):
        copy = (y + j) % NY * NZ + z
        mine.append(place_ref[copy])
        second = jnp.logical_and(place_ref[copy] == place_ref[copy ^ 1], copy % 2 == 1)
        primary.append(jnp.logical_not(second))
        use_ref[j] = jnp.where(second, -2, place_ref[copy])
    masks, gates, ids = [], [], []
    for group in GROUPS:
        for s in group:
            block = meta_ref[(z + (s + NZ)) % NZ].astype(F32)
            names, weights = block[:topk], block[topk:]
            ids.append(names)
            for j in range(NY):
                hit = names == mine[j].astype(F32)
                masks.append(jnp.sum(jnp.where(hit, 1.0, 0.0), axis=0, keepdims=True))
                gates.append(jnp.sum(jnp.where(hit, weights, 0.0), axis=0, keepdims=True))
    first = lax.broadcasted_iota(jnp.int32, (tok, tok), 0)
    before = jnp.where(first < lax.broadcasted_iota(jnp.int32, (tok, tok), 1), 1.0, 0.0).astype(BF)
    mask = jnp.concatenate(masks, axis=0)
    position = jnp.dot(mask.astype(BF), before, preferred_element_type=F32)
    order = [s for group in GROUPS for s in group]

    def rows_of(i, n):
        chosen = mask[NY * i : NY * (i + 1)] > 0.0
        return jnp.where(chosen, position[NY * i : NY * (i + 1)] + float(stride * n), -1.0)

    refs = list(rows_refs)
    for group in GROUPS:
        dest_ref = refs.pop(0)
        for n, s in enumerate(group):
            i = order.index(s)
            dest = rows_of(i, n)
            dest_ref[:, tok * n : tok * (n + 1)] = dest
            gate = gates[NY * i : NY * (i + 1)]
            kept = [jnp.where(primary[j], gate[j], 0.0) for j in range(NY)]
            pad = jnp.full((EXTRA // 2 - topk - 2 * NY, tok), -1.0, F32)
            tall = jnp.concatenate([ids[i], dest, *kept, pad, ids[i], dest, *kept, pad], axis=0)
            table_ref[tok * i : tok * (i + 1), :] = tall.T
    for group in DY_GROUPS:
        dest_ref, gate_ref = refs.pop(0), refs.pop(0)
        for n, s in enumerate(group):
            i = order.index(s)
            dest_ref[:, tok * n : tok * (n + 1)] = rows_of(i, n)
            gate_ref[:, tok * n : tok * (n + 1)] = jnp.concatenate(gates[NY * i : NY * (i + 1)], axis=0)


def route(at, placement, meta, stride, topk):
    tok = meta.shape[2]
    smem, vmem = pl.BlockSpec(memory_space=pltpu.SMEM), pl.BlockSpec(memory_space=pltpu.VMEM)
    shapes = [jax.ShapeDtypeStruct((NY,), jnp.int32), jax.ShapeDtypeStruct((NZ * tok, EXTRA), F32)]
    for group in GROUPS:
        shapes += [jax.ShapeDtypeStruct((NY, len(group) * tok), F32)]
    for group in DY_GROUPS:
        shapes += [jax.ShapeDtypeStruct((NY, len(group) * tok), F32)] * 2
    return pl.pallas_call(
        lambda *refs: route_kernel(stride, topk, *refs),
        in_specs=[smem, smem, vmem],
        out_specs=[smem] + [vmem] * (len(shapes) - 1),
        out_shape=shapes,
        name="route",
    )(at, placement, meta)


def dispatch_kernel(stride, tok, scaled, parts, units, *refs):
    refs = list(refs)
    dest_ref = refs.pop(0)
    gate_ref = refs.pop(0) if scaled else None
    sources = [stacked([refs.pop(0)[...] for _ in range(n)]) for n in parts]
    outs, plains = refs[:NY], refs[NY:]
    at = 0
    for n in units:
        rows = (lax.broadcasted_iota(jnp.int32, (n * stride, n * tok), 0) + stride * at).astype(F32)
        cols = slice(tok * at, tok * (at + n))
        picks, gated = [], []
        for j in range(NY):
            hit = rows == dest_ref[j : j + 1, cols]
            picks.append(jnp.where(hit, 1.0, 0.0))
            if scaled:
                gate = jnp.broadcast_to(gate_ref[j : j + 1, cols], hit.shape)
                gated.append(jnp.where(hit, gate, 0.0))
        got = jnp.dot(
            jnp.concatenate(gated + picks, axis=0).astype(BF),
            stacked(sources[at : at + n]),
            preferred_element_type=F32,
        )
        for i, out in enumerate(outs + plains):
            out[stride * at : stride * (at + n), :] = got[n * stride * i : n * stride * (i + 1), :].astype(BF)
        at += n


def dispatch(sources, units, dest, stride, tok, gate=None):
    scaled = gate is not None
    width = sources[0][0].shape[1]
    flat = [v for s in sources for v in s]
    wide = 512 if width % 512 == 0 else width
    small = pl.BlockSpec(dest.shape, lambda i: (0, 0))
    count = 2 * NY if scaled else NY
    rows = len(sources) * stride
    return pl.pallas_call(
        lambda *refs: dispatch_kernel(stride, tok, scaled, [len(s) for s in sources], units, *refs),
        grid=(width // wide,),
        in_specs=[small] * (1 + scaled) + [pl.BlockSpec((v.shape[0], wide), lambda i: (0, i)) for v in flat],
        out_specs=[pl.BlockSpec((rows, wide), lambda i: (0, i))] * count,
        out_shape=[jax.ShapeDtypeStruct((rows, width), BF)] * count,
        name="dispatch_scaled" if scaled else "dispatch",
    )(dest, *([gate] if scaled else []), *flat)


def forward_kernel(count, *refs):
    xs, (gu_ref, d_ref), outs = refs[:count], refs[count : count + 2], refs[count + 2 : 2 * count + 2]
    proj_ref, hidden_ref = refs[2 * count + 2 :]
    ff = d_ref.shape[0]
    x = stacked([ref[...] for ref in xs])
    proj = jnp.dot(x, gu_ref[...], preferred_element_type=F32)
    proj_ref[...] = proj
    pre_gate = proj[:, :ff]
    hidden = pre_gate * jax.nn.sigmoid(pre_gate) * proj[:, ff:]
    hidden_ref[...] = hidden.T.astype(BF)
    out = jnp.dot(hidden.astype(BF), d_ref[...], preferred_element_type=F32)
    at = 0
    for ref in outs:
        ref[...] = out[at : at + ref.shape[0], :].astype(BF)
        at += ref.shape[0]


def forward(xs, w_gu, w_d):
    rows = sum(x.shape[0] for x in xs)
    ff = w_d.shape[0]
    return pl.pallas_call(
        lambda *refs: forward_kernel(len(xs), *refs),
        out_shape=[jax.ShapeDtypeStruct(x.shape, BF) for x in xs]
        + [jax.ShapeDtypeStruct((rows, 2 * ff), F32), jax.ShapeDtypeStruct((ff, rows), BF)],
        name="forward",
    )(*xs, w_gu, w_d)


def slope_kernel(*refs):
    dys, (d_ref, proj_ref, out_ref) = refs[:NY], refs[NY:]
    ff = d_ref.shape[0]
    dy = stacked([ref[...] for ref in dys])
    d_hidden = lax.dot_general(dy, d_ref[...], (((1,), (1,)), ((), ())), preferred_element_type=F32)
    pre_gate = proj_ref[:, :ff]
    sig = jax.nn.sigmoid(pre_gate)
    out_ref[:ff, :] = (d_hidden * proj_ref[:, ff:] * (sig * (1.0 + pre_gate * (1.0 - sig)))).T.astype(BF)
    out_ref[ff:, :] = (d_hidden * (pre_gate * sig)).T.astype(BF)


def slopes(dys, w_d, proj):
    return pl.pallas_call(
        slope_kernel,
        out_shape=jax.ShapeDtypeStruct(proj.shape[::-1], BF),
        name="slopes",
    )(*dys, w_d, proj)


def grads_kernel(counts, at_ref, *refs):
    refs = list(refs)
    xs, dys = ([[refs.pop(0) for _ in range(n)] for n in side] for side in counts)
    das, hs = ([refs.pop(0) for _ in side] for side in counts)
    out_ref = refs.pop(0)
    cut = das[0].shape[0]
    for left, right, lo, hi in ((das, xs, 0, cut), (hs, dys, cut, out_ref.shape[1])):
        total = None
        for lhs, rhs in zip(left, right):
            part = jnp.dot(lhs[...], stacked([ref[...] for ref in rhs]), preferred_element_type=F32)
            total = part if total is None else total + part
        out_ref[0, lo:hi, :] = total.astype(out_ref.dtype)


def grads(at, flip, devices, xs, dys, das, hs, tile):
    steps = devices // 2
    rows = das[0].shape[0] + hs[0].shape[0]
    counts = [[len(v) for v in side] for side in (xs, dys)]
    flat = [v for side in (xs, dys) for vs in side for v in vs]
    moving = [pl.BlockSpec((v.shape[0], tile), lambda i, o: (0, (o[2] + 2 * i) % devices ^ flip)) for v in flat]
    fixed = [pl.BlockSpec(v.shape, lambda i, o: (0, 0)) for v in das + hs]
    return pl.pallas_call(
        lambda *refs: grads_kernel(counts, *refs),
        grid_spec=pltpu.PrefetchScalarGridSpec(
            num_scalar_prefetch=1,
            grid=(steps,),
            in_specs=moving + fixed,
            out_specs=pl.BlockSpec((1, rows, tile), lambda i, o: (i, 0, 0)),
        ),
        out_shape=jax.ShapeDtypeStruct((steps, rows, tile), BF),
        name="grads",
    )(at, *flat, *das, *hs)


def total_kernel(*refs):
    parts, gu_ref, d_ref = refs[:-2], refs[-2], refs[-1]
    ff = d_ref.shape[0]
    total = parts[0][0].astype(F32) + parts[1][0].astype(F32)
    for ref in parts[2:]:
        total = total + ref[...].astype(F32)
    both = total[: 2 * ff, :].T
    gu_ref[:, 0, :] = both[:, :ff]
    gu_ref[:, 1, :] = both[:, ff:]
    d_ref[...] = total[2 * ff :, :]


def totals(keep, taken, parts, ff):
    _, rows, tile = keep.shape
    first = pl.BlockSpec((1, rows, tile), lambda i: (0, 0, 0))
    return pl.pallas_call(
        total_kernel,
        grid=(1,),
        in_specs=[first, first] + [pl.BlockSpec((rows, tile), lambda i: (0, 0))] * len(parts),
        out_specs=[pl.BlockSpec((tile, 2, ff), lambda i: (0, 0, 0)), pl.BlockSpec((ff, tile), lambda i: (0, 0))],
        out_shape=[jax.ShapeDtypeStruct((tile, 2, ff), F32), jax.ShapeDtypeStruct((ff, tile), F32)],
        name="total",
    )(keep, taken, *parts)


def combine_kernel(stride, tok, topk, start, first, skip, units, came, *refs):
    use_ref, table_ref = refs[:2]
    backs, plains = refs[2 : 2 + NY], refs[2 + NY : 2 + 2 * NY]
    arrived, outs = refs[2 + 2 * NY : 2 + 2 * NY + came], refs[2 + 2 * NY + came :]
    width = backs[0].shape[1]
    base, rows = stride * first, stride * sum(units)
    wide = 512 if width % 512 == 0 else width
    lanes = lax.broadcasted_iota(jnp.int32, (rows, EXTRA), 1)
    sums = []
    for j in range(NY):

        def dotted(c, part):
            at = pl.ds(pl.multiple_of(c * 128, 128), 128)
            back, plain = backs[j][base : base + rows, at], plains[j][skip + base : skip + base + rows, at]
            return part + back.astype(F32) * plain.astype(F32)

        part = lax.fori_loop(0, width // 128, dotted, jnp.zeros((rows, 128), F32))
        val = jnp.sum(part, axis=1, keepdims=True)
        high = val.astype(BF).astype(F32)
        sums.append(jnp.where(lanes == j, high, jnp.where(lanes == j + NY, val - high, 0.0)))
    at = 0
    for n in units:
        low, size, count = stride * at, stride * n, tok * n
        from_ = tok * (start + first + at)
        table = table_ref[from_ : from_ + count, :]
        cols = lax.broadcasted_iota(jnp.int32, (count, NY * size), 1).astype(F32)
        weights = jnp.zeros((count, NY * size), F32)
        picks = jnp.zeros((count, NY * size), F32)
        for j in range(NY):
            dest = table[:, topk + j : topk + j + 1]
            dest = jnp.where(dest >= 0.0, dest + float(size * j - low - base), -1.0)
            hit = cols == dest
            weights = jnp.where(hit, table[:, topk + NY + j : topk + NY + j + 1], weights)
            picks = jnp.where(hit, 1.0, picks)
        weights = weights.astype(BF)
        dots = jnp.dot(
            picks.astype(BF),
            jnp.concatenate([v[low : low + size] for v in sums], axis=0).astype(BF),
            preferred_element_type=F32,
        )
        value = jnp.zeros((count, EXTRA), F32)
        for j in range(NY):
            dot = dots[:, j : j + 1] + dots[:, NY + j : NY + j + 1]
            value = jnp.where(table == use_ref[j].astype(F32), dot, value)
        high = value.astype(BF).astype(F32)
        lane = lax.broadcasted_iota(jnp.int32, (count, EXTRA), 1)
        value = jnp.where(lane % (EXTRA // 2) < topk, jnp.where(lane < EXTRA // 2, high, value - high), 0.0)

        def write(place, block):
            for i in range(n):
                piece = block[tok * i : tok * (i + 1), :]
                if at + i < came:
                    piece = piece + arrived[at + i][:, place].astype(F32)
                outs[at + i][:, place] = piece.astype(BF)

        def mixed(c, _):
            place = pl.ds(pl.multiple_of(c * wide, 128), wide)
            rhs = stacked([back[base + low : base + low + size, place] for back in backs])
            write(place, jnp.dot(weights, rhs, preferred_element_type=F32))
            return _

        write(slice(width, width + EXTRA), value)
        lax.fori_loop(0, width // wide, mixed, 0)
        at += n


def combine(use, table, backs, plains, stride, tok, topk, start, first, skip, units, arrived=()):
    width = backs[0].shape[1]
    smem, vmem = pl.BlockSpec(memory_space=pltpu.SMEM), pl.BlockSpec(memory_space=pltpu.VMEM)
    return pl.pallas_call(
        lambda *refs: combine_kernel(stride, tok, topk, start, first, skip, units, len(arrived), *refs),
        in_specs=[smem] + [vmem] * (1 + 2 * NY + len(arrived)),
        out_shape=[jax.ShapeDtypeStruct((tok, width + EXTRA), BF)] * sum(units),
        name="combine",
    )(use, table, *backs, *plains, *arrived)


def plus(*values):
    return sum(v.astype(F32) for v in values)


def on_device(tokens, cotangent, gates, expert_ids, placement, gate_up, down):
    tok, width = tokens.shape
    topk = expert_ids.shape[1]
    copies = placement.shape[0]
    experts = copies - copies // 8
    capacity = tok * topk * 17 // (16 * experts) + 1
    stride = (capacity + 7) // 8 * 8
    ff = down.shape[1]
    at = jnp.stack([lax.axis_index(name).astype(jnp.int32) for name in ("ey", "ez", "dp")])

    meta = jnp.concatenate([expert_ids.T.astype(BF), gates.T], axis=0)
    meta_all = lax.all_to_all(
        jnp.broadcast_to(meta[None], (NZ,) + meta.shape), "ez", split_axis=0, concat_axis=0, tiled=True
    )
    meta_all, w_gu = lax.optimization_barrier((meta_all, gate_up[0].reshape(width, 2 * ff)))
    x_ring = gather_ring(tokens, True)
    y_ring = gather_ring(cotangent, False)
    use, table, *rows = route(at, placement, meta_all, stride, topk)
    dests, dy_rows = rows[: len(GROUPS)], rows[len(GROUPS) :]
    w_d = down[0]

    def sent_over_y(blocks, sign):
        out = [blocks[0]]
        for j in range(1, NY):
            out.append(shifted(blocks[j], "ey", sign * j))
        return out

    blocks, backs = [], [None] * len(GROUPS)
    for g, group in enumerate(GROUPS):
        sent = dispatch([x_ring[s] for s in group], UNITS[g], dests[g], stride, tok)
        blocks.append(sent_over_y(sent, 1))
    xs, dys, plains, hs, das = [], [], [], [], []
    for n, stage in enumerate(STAGES):
        sent = dispatch([y_ring[s] for s in DY_GROUPS[n]], DY_UNITS[n], dy_rows[2 * n], stride, tok, dy_rows[2 * n + 1])
        plains.append(sent[NY:])
        dys.append(sent_over_y(sent, 1))
        xs.append([blocks[g][j] for j in range(NY) for g in stage])
        *outs, proj, hidden = forward(xs[n], w_gu, w_d)
        hs.append(hidden)
        for i, g in enumerate(stage):
            backs[g] = sent_over_y(outs[i :: len(stage)], -1)
        das.append(slopes(dys[n], w_d, proj))

    devices = lax.axis_size("dp")
    tile = width // devices
    turns = devices // 2
    every = xs, dys, das, hs, tile
    give = grads(at, 1, devices, *every)
    taken = lax.ppermute(give, "dp", [(i, i ^ 1) for i in range(devices)])
    keep = grads(at, 0, devices, *every)
    parts = []
    for k in range(1, turns):
        parts.append(shifted(plus(keep[k], taken[k]).astype(BF), "dp", 2 * k))
    total_gu, total_d = totals(keep, taken, parts, ff)

    def hop(up, down_):
        return shifted(up, "ez", -1), shifted(down_, "ez", 1)

    def partials(g, plain, first, skip, units, arrived=()):
        start = sum(len(group) for group in GROUPS[:g])
        return combine(use, table, backs[g], plain, stride, tok, topk, start, first, skip, units, arrived)

    up, down_, far = partials(2, plains[1], 0, 0, UNITS[2])
    up, down_ = hop(up, down_)
    far = shifted(far, "ez", 4)
    up, down_ = hop(*partials(1, plains[0], 0, 0, UNITS[1], (up, down_)))
    up, down_ = hop(*partials(0, plains[0], 0, 2 * stride, UNITS[0][:1], (up, down_)))
    (own,) = partials(0, plains[0], 2, 2 * stride, UNITS[0][1:])
    whole = plus(own, far, up, down_)
    mixed = whole[:, :width].astype(BF)
    extra = whole[:, width:]
    d_gates = extra[:, :topk] + extra[:, EXTRA // 2 : EXTRA // 2 + topk]
    return (
        mixed,
        d_gates,
        total_gu[None],
        total_d[None],
    )


def solution(mesh):
    split = Mesh(mesh.devices.reshape(mesh.shape["dp"], NY, NZ), ("dp", "ey", "ez"))
    tokens = P(("dp", "ey", "ez"), None)
    return jax.shard_map(
        on_device,
        mesh=split,
        in_specs=(
            tokens,
            tokens,
            tokens,
            tokens,
            P(),
            P(("ey", "ez"), None, None, None),
            P(("ey", "ez"), None, None),
        ),
        out_specs=(
            tokens,
            tokens,
            P(("ey", "ez"), "dp", None, None),
            P(("ey", "ez"), None, "dp"),
        ),
        check_vma=False,
    )
```
